32 devices in a mesh: chan: 4 (over x, core), pix: 8 (over z, y).
Axes of the slice: x: 2, y: 2, z: 4, core: 2. Of those that a mesh axis runs over, the one named last changes fastest.
Arguments:
- sky_map: bfloat16 [1024, 256, 1024], P('chan', 'pix'), may hold values from -6 to 6
- owner: int32 [256], P('pix'), may hold values from -1 to 3, as said below
- stamp_block: int32 [8, 4, 8, 2], P('pix', 'chan'), may hold values from -1 to 5, as said below
- chan_start: int32 [8, 4, 8, 2], P('pix', 'chan'), may hold values from 0 to 896
- overdensity: float32 [8, 4, 8, 2], replicated, may hold values from 0.2 to 3
- delay_gain: float32 [1024], replicated, may hold values from 0.1 to 1
Outputs:
- stack: float32 [8, 128, 1024], P('pix', 'chan')
The draws below stay inside these ranges and needn't reach their ends.
Inputs may be any that keep to these rules, and one draw needn't show every extreme that they name: `owner`: within each strip column every index 0 to 3 owns between 1 and 6 blocks, some index exactly 6; -1 marks masked blocks. `stamp_block`: A listed rank is below the number of blocks that the list's index owns in the list's strip column; -1 marks an empty slot; for some shard every list fills all 2 slots.
All inputs are finite; a program needn't handle non-finite values.
Results may differ from the reference program's by a relative error of at most 0.0043.
Values may be sent and summed in bfloat16 or wider, within the bound.
A program may use at most 128 MiB of HBM per device.

```python
import math
import jax
import jax.numpy as jnp
from jax import lax

CH = 1024
PIX = 1024
SCH = 128
BLK_DEV = 32
SCAP = 2
CAP = 6
NBLK = 256
N_CHAN = 4
N_PIX = 8


def layout(key):
    base_key = jax.random.fold_in(key, 11)
    full_shard = jax.random.randint(jax.random.fold_in(base_key, 1), (), 0, N_PIX)

    def one_source(source):
        source_key = jax.random.fold_in(base_key, 100 + source)
        key_count, key_heavy, key_order, key_fill, key_chosen = jax.random.split(source_key, 5)
        counts = jax.random.randint(key_count, (N_CHAN,), 1, CAP + 1)
        heavy_owner = jax.random.randint(key_heavy, (), 0, N_CHAN)
        counts = jnp.where(jnp.arange(N_CHAN) == heavy_owner, CAP, counts).astype(jnp.int32)
        rank_ends = jnp.cumsum(counts).astype(jnp.int32)
        block_order = jax.random.permutation(key_order, BLK_DEV).astype(jnp.int32)
        ranks = jnp.arange(BLK_DEV, dtype=jnp.int32)
        holder = jnp.sum((rank_ends[None, :] <= ranks[:, None]).astype(jnp.int32), axis=1)
        holder = jnp.where(ranks < rank_ends[-1], holder, -1).astype(jnp.int32)
        owner_local = jnp.zeros((BLK_DEV,), jnp.int32).at[block_order].set(holder)
        filled = jax.random.randint(key_fill, (N_CHAN, N_PIX), 0, SCAP + 1)
        filled = jnp.where(jnp.arange(N_PIX)[None, :] == full_shard, SCAP, filled)
        chosen = jax.random.randint(key_chosen, (N_CHAN, N_PIX, SCAP), 0, 65536) % counts[:, None, None]
        chosen = chosen.at[heavy_owner, full_shard, 0].set(CAP - 1)
        live_slot = jnp.arange(SCAP)[None, None, :] < filled[:, :, None]
        return (owner_local, jnp.where(live_slot, chosen, -1).astype(jnp.int32))
    owners, block_lists = jax.vmap(one_source)(jnp.arange(N_PIX))
    return (owners.reshape(-1), block_lists)


def draw_owner(key, part):
    return layout(key)[0]


def draw_stamp_block(key, part):
    return layout(key)[1]


def draw_chan_start(key, part):
    shape = (N_PIX, N_CHAN, N_PIX, SCAP)
    starts = jax.random.randint(jax.random.fold_in(key, 23), shape, 0, CH - SCH + 1).astype(jnp.int32)
    starts = starts.at[0, 0, 0, 0].set(CH - SCH)
    return starts.at[N_PIX - 1, N_CHAN - 1, N_PIX - 1, SCAP - 1].set(0)


def shard_levels(stream_key, shape, cuts, least, high):
    def one(position, blocks):
        heights = jax.random.uniform(jax.random.fold_in(jax.random.fold_in(stream_key, 6), position), (blocks,), jnp.float32, least / len(cuts), high / len(cuts))
        return jnp.repeat(jnp.exp(heights), shape[position] // blocks).reshape((-1,) + (1,) * (len(shape) - position - 1))

    level = one(*cuts[0])
    for cut in cuts[1:]:
        level = level * one(*cut)
    return level


def centred(own_key, dims, width, most, cuts=(), kind=jnp.bfloat16):
    drawn = width * jax.random.normal(own_key, dims, jnp.float32)
    if cuts:
        drawn = drawn * shard_levels(own_key, dims, cuts, -0.22, 0.18)
    return jnp.clip(drawn, -most, most).astype(kind)


def setup_inputs(seed: int = 0) -> dict:
    key_list = jax.random.split(jax.random.key(seed), 7)
    return {
        "sky_map": centred(key_list[0], (CH, NBLK, PIX), 1.0, 6.0, ((0, 4), (1, 8))),
        "owner": draw_owner(jax.random.fold_in(key_list[6], 71), 0),
        "stamp_block": draw_stamp_block(jax.random.fold_in(key_list[6], 71), 0),
        "chan_start": draw_chan_start(jax.random.fold_in(key_list[6], 71), 0),
        "overdensity": jnp.clip(jax.random.uniform(key_list[4], (N_PIX, N_CHAN, N_PIX, SCAP), jnp.float32, 0.2, 3.0), 0.2, 3.0),
        "delay_gain": jnp.clip(jnp.exp(jax.random.uniform(key_list[5], (CH,), jnp.float32, math.log(0.1), math.log(1.0))), 0.1, 1.0),
    }


def delay_table(size):
    mode = jnp.arange(size, dtype=jnp.int32)[:, None]
    chan_index = jnp.arange(size, dtype=jnp.int32)[None, :]
    half = size // 2
    freq = jnp.where(mode <= half, mode, mode - half)
    phase = freq * chan_index % size
    angle = phase.astype(jnp.float32) * (2.0 * math.pi / size)
    edge = 1.0 / math.sqrt(size)
    inner = math.sqrt(2.0 / size)
    return jnp.where(mode == 0, edge + 0.0 * angle, jnp.where(mode == half, edge * jnp.cos(angle), jnp.where(mode < half, inner * jnp.cos(angle), inner * jnp.sin(angle))))

def reference(sky_map, owner, stamp_block, chan_start, overdensity, delay_gain):
    basis = delay_table(CH)
    filter_matrix = jnp.dot((basis * delay_gain[:, None]).T, basis, precision=lax.Precision.HIGHEST, preferred_element_type=jnp.float32).astype(jnp.bfloat16)
    source_maps = sky_map.reshape(CH, N_PIX, BLK_DEV, PIX)
    owner_cols = owner.reshape(N_PIX, BLK_DEV)
    wide_filter = filter_matrix.astype(jnp.float32)
    block_ids = jnp.arange(BLK_DEV, dtype=jnp.int32)
    chan_ids = jnp.arange(N_CHAN, dtype=jnp.int32)

    def one_source(total, source):
        column = lax.dynamic_index_in_dim(source_maps, source, 1, False)
        owner_col = lax.dynamic_index_in_dim(owner_cols, source, 0, False)
        same_owner = owner_col[:, None] == owner_col[None, :]
        earlier = block_ids[None, :] < block_ids[:, None]
        block_rank = lax.optimization_barrier(jnp.sum((same_owner & earlier).astype(jnp.int32), axis=1))
        filtered = jnp.einsum('mk,kbp->mbp', wide_filter, column.astype(jnp.float32)).astype(jnp.bfloat16)
        rank_lists = lax.dynamic_index_in_dim(stamp_block, source, 0, False)
        first_chan = lax.dynamic_index_in_dim(chan_start, source, 0, False)
        weights = lax.dynamic_index_in_dim(overdensity, source, 0, False)
        match = (owner_col[None, None, None, :] == chan_ids[:, None, None, None]) & (block_rank[None, None, None, :] == rank_lists[:, :, :, None])
        live_slot = jnp.any(match, axis=3) & (rank_lists >= 0)
        block_index = lax.optimization_barrier(jnp.sum(jnp.where(match, block_ids[None, None, None, :], 0), axis=3)).astype(jnp.int32)

        def cut_stamp(block_one, chan_one):
            start = (chan_one.astype(jnp.int32), block_one.astype(jnp.int32), jnp.int32(0))
            return lax.dynamic_slice(filtered, start, (SCH, 1, PIX))[:, 0, :]
        stamps = jax.vmap(jax.vmap(jax.vmap(cut_stamp)))(block_index, first_chan)
        weights = jnp.where(live_slot, weights, 0.0)
        return (total + jnp.einsum('cqs,cqskp->qkp', weights.astype(jnp.float32), stamps.astype(jnp.float32)), None)
    start_total = jnp.zeros((N_PIX, SCH, PIX), jnp.float32)
    stack, unused = lax.scan(one_source, start_total, jnp.arange(N_PIX, dtype=jnp.int32))
    return stack
```

```python
import functools

import jax
import jax.numpy as jnp
import numpy as np
from jax import lax
from jax.experimental import pallas as pl
from jax.experimental.pallas import tpu as pltpu
from jax.sharding import PartitionSpec as P

MESH = pl.DeviceIdType.MESH
LANES = 128
TILE = 256
GROUP = 4
LAG1 = 2
LAG2 = 6


def angle_tables(size):
    half = size // 2
    mode = np.arange(half)
    coarse = 2.0 * np.pi * ((mode[None, :] * np.arange(size // LANES)[:, None] * LANES) % size) / size
    fine = 2.0 * np.pi * ((mode[:, None] * np.arange(LANES)[None, :]) % size) / size
    left = np.concatenate([np.cos(coarse), -np.sin(coarse)], axis=1)
    right = np.concatenate([np.cos(fine), np.sin(fine)], axis=0) / size
    return left.astype(np.float32), right.astype(np.float32)


def filter_kernels(gain, coarse, fine):
    size = gain.shape[1]
    half = size // 2
    lanes = size // LANES
    even = gain[:, :half]
    odd = gain[:, half:]
    mode = lax.broadcasted_iota(jnp.int32, (1, half), 1)
    odd = jnp.where(mode == 0, 0.0, odd)
    plus = even + odd
    minus = jnp.where(mode == 0, 0.0, even - odd)
    plus = jnp.concatenate([plus, plus], axis=1)
    minus = jnp.concatenate([minus, minus], axis=1)
    left = jnp.concatenate([coarse * plus, coarse * minus], axis=0)
    out = jnp.dot(left, fine, precision=lax.Precision.HIGHEST, preferred_element_type=jnp.float32)
    sign = jnp.where(lax.rem(lax.broadcasted_iota(jnp.int32, (1, LANES), 1), 2) == 0, 1.0 / size, -1.0 / size)
    last = gain[:, half : half + 1] * sign
    diff = [jnp.broadcast_to(out[a : a + 1] + last, (8, LANES)) for a in range(lanes)]
    add = [jnp.broadcast_to(out[lanes + a : lanes + a + 1], (8, LANES)) for a in range(lanes)]
    return jnp.concatenate(diff, axis=1), jnp.concatenate(add, axis=1)


def fill_filter(first, diff, add, filt):
    size = diff.shape[1]
    halves = filt.shape[0]
    row = lax.broadcasted_iota(jnp.int32, (8, size), 0)
    back = lax.rem(size - first, size)
    diff = pltpu.roll(diff, back, 1)
    add = pltpu.roll(add, back, 1)
    diff_rows, add_rows = diff, add
    for i in range(1, 8):
        diff_rows = jnp.where(row == i, pltpu.roll(diff, i, 1), diff_rows)
        add_rows = jnp.where(row == i, pltpu.roll(add, size - i, 1), add_rows)
    lanes = size // LANES
    for v in range(LANES // 8):
        right = pltpu.roll(diff_rows, 8 * v, 1) if v else diff_rows
        left = pltpu.roll(add_rows, size - 8 * v, 1) if v else add_rows
        for u in range(lanes):
            for h in range(halves):
                a = (h - u) % lanes
                b = (h + u) % lanes
                rows = right[:, a * LANES : (a + 1) * LANES] + left[:, b * LANES : (b + 1) * LANES]
                rows = rows.astype(jnp.bfloat16).astype(jnp.float32)
                filt[h, u * LANES + 8 * v : u * LANES + 8 * v + 8, :] = rows


def resolve(c, owner, ranks, starts, lists):
    blocks = owner.shape[1]
    slots, shards = ranks.shape
    row = lax.broadcasted_iota(jnp.int32, (blocks, blocks), 0)
    col = lax.broadcasted_iota(jnp.int32, (blocks, blocks), 1)
    across = jnp.broadcast_to(owner, (blocks, blocks))
    down = jnp.sum(jnp.where(row == col, across, 0), axis=1, keepdims=True)
    rank = jnp.sum(jnp.where((across == c) & (col < row), 1, 0), axis=1, keepdims=True)
    rank = jnp.where(down == c, rank, -2)
    number = lax.broadcasted_iota(jnp.int32, (blocks, shards), 0) + 1
    lists[...] = jnp.zeros_like(lists)
    for s in range(slots):
        match = jnp.broadcast_to(rank, (blocks, shards)) == jnp.broadcast_to(ranks[s : s + 1], (blocks, shards))
        lists[s : s + 1, :shards] = jnp.sum(jnp.where(match, number, 0), axis=0, keepdims=True) - 1
    lists[slots : 2 * slots, :shards] = starts


def stack_kernel(
    groups, shards, slots, stamp, owner_ref, ranks_ref, starts_ref, over_ref, gain_ref, coarse_ref, fine_ref, sky_ref, out_ref,
    owner, ranks, starts, over, gain, coarse, fine, arg_sem, raw, sky_sem, lists, lists_s, over_v, over_s, local, send_l, recv_l,
    held, filt, cuts, part, kept, pair, mid1, near, keep, mid2, own, far, send0, recv0, send1, recv1, send2, recv2,
):
    chunks, width, blocks, tile = raw.shape
    chips = groups // 2
    rows = stamp // groups
    each = shards // GROUP
    steps = chunks * GROUP
    cut_rows = width // GROUP
    k = lax.axis_index("chan")
    p = lax.axis_index("pix")
    x = k // 2
    core = lax.rem(k, 2)
    other = 1 - core

    def fetch(t):
        n, j = t // GROUP, lax.rem(t, GROUP)
        lane = pl.multiple_of(n * tile, tile)
        here = pl.multiple_of(j * cut_rows, cut_rows)
        return pltpu.make_async_copy(
            sky_ref.at[pl.ds(here, cut_rows), :, pl.ds(lane, tile)], raw.at[n, pl.ds(here, cut_rows)], sky_sem.at[t]
        )

    sources = (owner_ref, ranks_ref, starts_ref, over_ref.at[p], gain_ref, coarse_ref, fine_ref)
    targets = (owner, ranks, starts, over, gain, coarse, fine)
    args = [pltpu.make_async_copy(a, b, arg_sem.at[i]) for i, (a, b) in enumerate(zip(sources, targets))]

    barrier = pltpu.get_barrier_semaphore()
    for e in range(1, groups):
        pl.semaphore_signal(barrier, inc=1, device_id=(lax.rem(k + e, groups), p), device_id_type=MESH)
    for d in range(1, shards):
        pl.semaphore_signal(barrier, inc=1, device_id=(k, lax.rem(p + d, shards)), device_id_type=MESH)
    for copy in args:
        copy.start()

    @pl.loop(0, steps)
    def _(t):
        fetch(t).start()

    def to_peer(e):
        return pltpu.make_async_remote_copy(
            src_ref=lists.at[0],
            dst_ref=lists.at[e],
            send_sem=send_l.at[e - 1],
            recv_sem=recv_l.at[e - 1],
            device_id=(lax.rem(k + e, groups), p),
            device_id_type=MESH,
        )

    def transpose(t):
        n, j = t // GROUP, lax.rem(t, GROUP)
        fetch(t).wait()

        @pl.loop(0, cut_rows // 16)
        def _(i):
            here = pl.multiple_of(j * cut_rows + 16 * i, 16)
            for b in range(0, blocks, 16):
                held[n, b : b + 16, pl.ds(here, 16), :] = jnp.swapaxes(raw[n, pl.ds(here, 16), b : b + 16, :], 0, 1)

    def to_core(t):
        return pltpu.make_async_remote_copy(
            src_ref=part.at[t],
            dst_ref=pair.at[t],
            send_sem=send0.at[t],
            recv_sem=recv0.at[t],
            device_id=(x * 2 + other, p),
            device_id_type=MESH,
        )

    def to_chip(t, j):
        return pltpu.make_async_remote_copy(
            src_ref=mid1.at[t, j - 1],
            dst_ref=near.at[t, j - 1],
            send_sem=send1.at[t, j - 1],
            recv_sem=recv1.at[t, j - 1],
            device_id=(lax.rem(x + j, chips) * 2 + core, p),
            device_id_type=MESH,
        )

    def to_shard(t, r):
        d = 1 + lax.rem(t, GROUP) * each + r
        return pltpu.make_async_remote_copy(
            src_ref=mid2.at[t, r],
            dst_ref=far.at[t, r],
            send_sem=send2.at[t, r],
            recv_sem=recv2.at[t, r],
            device_id=(k, lax.rem(p + d, shards)),
            device_id_type=MESH,
        )

    def compute(t):
        n, j = t // GROUP, lax.rem(t, GROUP)
        for r in range(each):
            i = j * each + r
            q = lax.rem(p + 1 + i, shards)
            found = [held[n, jnp.maximum(lists_s[e, s, q], 0)] for e in range(groups) for s in range(slots)]
            total = jnp.dot(cuts[i], jnp.concatenate(found, axis=0), preferred_element_type=jnp.float32)
            total = total.reshape(chips, 2, rows, tile)
            kept[t, r] = jnp.where(core == 0, total[:, 0], total[:, 1])
            part[t, r] = jnp.where(core == 0, total[:, 1], total[:, 0]).astype(jnp.bfloat16)

    def chip_stage(t):
        to_core(t).wait_recv()
        for j in range(1, chips):
            to = lax.rem(x + j, chips)
            mid1[t, j - 1] = (kept[t, :, to] + pair[t, :, to].astype(jnp.float32)).astype(jnp.bfloat16)
            to_chip(t, j).start()
        keep[t] = kept[t, :, x] + pair[t, :, x].astype(jnp.float32)

    def shard_stage(t):
        total = keep[t]
        for j in range(1, chips):
            to_chip(t, j).wait_recv()
            total += near[t, j - 1].astype(jnp.float32)
        mid2[t] = total.astype(jnp.bfloat16)
        for r in range(each - 1):
            to_shard(t, r).start()

        @pl.when(lax.rem(t, GROUP) < GROUP - 1)
        def _():
            to_shard(t, each - 1).start()

        @pl.when(lax.rem(t, GROUP) == GROUP - 1)
        def _():
            own[t // GROUP] = total[each - 1]

    for copy in args:
        copy.wait()
    resolve(k, owner[...], ranks[...], starts[...], lists.at[0])
    for c in range(groups):
        over_v[c * slots : (c + 1) * slots, :shards] = over[c]
    over_copy = pltpu.make_async_copy(over_v, over_s, local.at[0])
    over_copy.start()
    diff, add = filter_kernels(gain[...], coarse[...], fine[...])
    fill_filter(k * width, diff, add, filt)
    pl.semaphore_wait(barrier, groups + shards - 2)
    for e in range(1, groups):
        to_peer(e).start()

    @pl.loop(0, GROUP)
    def _(t):
        transpose(t)

    for e in range(1, groups):
        to_peer(e).wait_recv()
    lists_copy = pltpu.make_async_copy(lists, lists_s, local.at[1])
    lists_copy.start()
    over_copy.wait()
    lists_copy.wait()

    @pl.loop(0, shards)
    def _(i):
        q = lax.rem(p + 1 + i, shards)
        for e in range(groups):
            c = lax.rem(k + groups - e, groups)
            for s in range(slots):
                first = lists_s[e, slots + s, q]
                weight = jnp.where(lists_s[e, s, q] >= 0, over_s[c * slots + s, q], 0.0)
                at = (e * slots + s) * width
                for h in range(width // LANES):
                    rows_h = weight * filt[h, pl.ds(first, stamp), :]
                    cuts[i, :, at + h * LANES : at + (h + 1) * LANES] = rows_h.astype(jnp.bfloat16)

    @pl.loop(0, steps + LAG2)
    def _(t):
        @pl.when(t < steps)
        def _():
            compute(t)
            to_core(t).start()

        @pl.when(t < steps - GROUP)
        def _():
            transpose(t + GROUP)

        @pl.when((t >= LAG1) & (t < steps + LAG1))
        def _():
            chip_stage(t - LAG1)

        @pl.when(t >= LAG2)
        def _():
            shard_stage(t - LAG2)

    @pl.loop(0, chunks)
    def _(n):
        total = own[n]
        for j in range(GROUP):
            for r in range(each - (j == GROUP - 1)):
                to_shard(n * GROUP + j, r).wait_recv()
                total += far[n * GROUP + j, r].astype(jnp.float32)
        out_ref[:, pl.ds(pl.multiple_of(n * tile, tile), tile)] = total

    for e in range(1, groups):
        to_peer(e).wait_send()

    @pl.loop(0, steps)
    def _(t):
        to_core(t).wait_send()
        for j in range(1, chips):
            to_chip(t, j).wait_send()
        for r in range(each - 1):
            to_shard(t, r).wait_send()

        @pl.when(lax.rem(t, GROUP) < GROUP - 1)
        def _():
            to_shard(t, each - 1).wait_send()


def body(sky_map, owner, stamp_block, chan_start, overdensity, delay_gain, *, groups, shards):
    width, blocks, pixels = sky_map.shape
    stamp = 128
    chips = groups // 2
    rows = stamp // groups
    slots = stamp_block.shape[3]
    size = delay_gain.shape[0]
    chunks = pixels // TILE
    steps = chunks * GROUP
    each = shards // GROUP
    left, right = angle_tables(size)

    dma = pltpu.SemaphoreType.DMA
    f32, bf16, i32 = jnp.float32, jnp.bfloat16, jnp.int32
    vmem = pltpu.VMEM
    out = pl.pallas_call(
        functools.partial(stack_kernel, groups, shards, slots, stamp),
        out_shape=jax.ShapeDtypeStruct((rows, pixels), f32),
        in_specs=[pl.BlockSpec(memory_space=pl.ANY)] * 8,
        out_specs=pl.BlockSpec(memory_space=pltpu.VMEM),
        scratch_shapes=[
            vmem((1, blocks), i32),
            vmem((slots, shards), i32),
            vmem((slots, shards), i32),
            vmem((groups, slots, shards), f32),
            vmem((1, size), f32),
            vmem(left.shape, f32),
            vmem(right.shape, f32),
            dma((7,)),
            vmem((chunks, width, blocks, TILE), bf16),
            dma((steps,)),
            vmem((groups, 8, LANES), i32),
            pltpu.SMEM((groups, 8, LANES), i32),
            vmem((max(8, groups * slots), LANES), f32),
            pltpu.SMEM((max(8, groups * slots), LANES), f32),
            dma((2,)),
            dma((groups - 1,)),
            dma((groups - 1,)),
            vmem((chunks, blocks, width, TILE), bf16),
            vmem((width // LANES, size, LANES), f32),
            vmem((shards, stamp, groups * slots * width), bf16),
            vmem((steps, each, chips, rows, TILE), bf16),
            vmem((steps, each, chips, rows, TILE), f32),
            vmem((steps, each, chips, rows, TILE), bf16),
            vmem((steps, chips - 1, each, rows, TILE), bf16),
            vmem((steps, chips - 1, each, rows, TILE), bf16),
            vmem((steps, each, rows, TILE), f32),
            vmem((steps, each, rows, TILE), bf16),
            vmem((chunks, rows, TILE), f32),
            vmem((steps, each, rows, TILE), bf16),
            dma((steps,)),
            dma((steps,)),
            dma((steps, chips - 1)),
            dma((steps, chips - 1)),
            dma((steps, each)),
            dma((steps, each)),
        ],
        compiler_params=pltpu.CompilerParams(
            collective_id=0, has_side_effects=True, vmem_limit_bytes=58 << 20
        ),
        name="stack_stamps",
    )(
        owner.reshape(1, blocks),
        stamp_block[0, 0].T,
        chan_start[0, 0].T,
        jnp.swapaxes(overdensity, 2, 3),
        delay_gain.reshape(1, size),
        left,
        right,
        sky_map,
    )
    return out[None]


def solution(mesh):
    in_specs = (
        P("chan", "pix", None),
        P("pix"),
        P("pix", "chan", None, None),
        P("pix", "chan", None, None),
        P(),
        P(),
    )
    run = functools.partial(body, groups=mesh.shape["chan"], shards=mesh.shape["pix"])
    return jax.shard_map(run, mesh=mesh, in_specs=in_specs, out_specs=P("pix", "chan", None), check_vma=False)
```

```python
import functools

import jax
import jax.numpy as jnp
import numpy as np
from jax import lax
from jax.experimental import pallas as pl
from jax.experimental.pallas import tpu as pltpu
from jax.sharding import PartitionSpec as P

MESH = pl.DeviceIdType.MESH
LANES = 128
TILE = 512
PRE = 1
LAG1 = 1
LAG2 = 5
LAG3 = 8


def angle_tables(size):
    half = size // 2
    mode = np.arange(half)
    coarse = 2.0 * np.pi * ((mode[None, :] * np.arange(size // LANES)[:, None] * LANES) % size) / size
    fine = 2.0 * np.pi * ((mode[:, None] * np.arange(LANES)[None, :]) % size) / size
    left = np.concatenate([np.cos(coarse), -np.sin(coarse)], axis=1)
    right = np.concatenate([np.cos(fine), np.sin(fine)], axis=0) / size
    return left.astype(np.float32), right.astype(np.float32)


def filter_kernels(gain, coarse, fine):
    size = gain.shape[1]
    half = size // 2
    lanes = size // LANES
    even = gain[:, :half]
    odd = gain[:, half:]
    mode = lax.broadcasted_iota(jnp.int32, (1, half), 1)
    odd = jnp.where(mode == 0, 0.0, odd)
    plus = even + odd
    minus = jnp.where(mode == 0, 0.0, even - odd)
    plus = jnp.concatenate([plus, plus], axis=1)
    minus = jnp.concatenate([minus, minus], axis=1)
    left = jnp.concatenate([coarse * plus, coarse * minus], axis=0)
    out = jnp.dot(left, fine, precision=lax.Precision.HIGHEST, preferred_element_type=jnp.float32)
    sign = jnp.where(lax.rem(lax.broadcasted_iota(jnp.int32, (1, LANES), 1), 2) == 0, 1.0 / size, -1.0 / size)
    last = gain[:, half : half + 1] * sign
    diff = [jnp.broadcast_to(out[a : a + 1] + last, (8, LANES)) for a in range(lanes)]
    add = [jnp.broadcast_to(out[lanes + a : lanes + a + 1], (8, LANES)) for a in range(lanes)]
    return jnp.concatenate(diff, axis=1), jnp.concatenate(add, axis=1)


def fill_filter(first, diff, add, filt):
    size = diff.shape[1]
    halves = filt.shape[0]
    row = lax.broadcasted_iota(jnp.int32, (8, size), 0)
    back = lax.rem(size - first, size)
    diff = pltpu.roll(diff, back, 1)
    add = pltpu.roll(add, back, 1)
    diff_rows, add_rows = diff, add
    for i in range(1, 8):
        diff_rows = jnp.where(row == i, pltpu.roll(diff, i, 1), diff_rows)
        add_rows = jnp.where(row == i, pltpu.roll(add, size - i, 1), add_rows)
    lanes = size // LANES
    for v in range(LANES // 8):
        right = pltpu.roll(diff_rows, 8 * v, 1) if v else diff_rows
        left = pltpu.roll(add_rows, size - 8 * v, 1) if v else add_rows
        for u in range(lanes):
            for h in range(halves):
                a = (h - u) % lanes
                b = (h + u) % lanes
                rows = right[:, a * LANES : (a + 1) * LANES] + left[:, b * LANES : (b + 1) * LANES]
                rows = rows.astype(jnp.bfloat16).astype(jnp.float32)
                filt[h, u * LANES + 8 * v : u * LANES + 8 * v + 8, :] = rows


def resolve(k, owner, ranks, starts, lists):
    blocks = owner.shape[1]
    groups, slots, shards = ranks.shape
    row = lax.broadcasted_iota(jnp.int32, (blocks, blocks), 0)
    col = lax.broadcasted_iota(jnp.int32, (blocks, blocks), 1)
    across = jnp.broadcast_to(owner[...], (blocks, blocks))
    down = jnp.sum(jnp.where(row == col, across, 0), axis=1, keepdims=True)
    number = lax.broadcasted_iota(jnp.int32, (blocks, shards), 0) + 1
    rank = jnp.sum(jnp.where((across == down) & (col < row), 1, 0), axis=1, keepdims=True)
    for e in range(groups):
        c = lax.rem(k + groups - e, groups)
        held = jnp.broadcast_to(jnp.where(down == c, rank, -2), (blocks, shards))
        for s in range(slots):
            match = held == jnp.broadcast_to(ranks[e, s : s + 1], (blocks, shards))
            lists[e, s : s + 1, :shards] = jnp.sum(jnp.where(match, number, 0), axis=0, keepdims=True) - 1
        lists[e, slots : 2 * slots, :shards] = starts[e]


def stack_kernel(
    groups, shards, slots, stamp, owner_ref, ranks_ref, starts_ref, over_ref, gain_ref, coarse_ref, fine_ref, sky_ref, out_ref,
    owner, ranks, starts, over, gain, coarse, fine, arg_sem, raw, sky_sem, lists, lists_s, over_v, over_s, local, send_l, recv_l,
    filt, cuts, part, kept, pair, mid1, near1, keep1, mid2, near2, keep2, last, far, own,
    send0, recv0, send1, recv1, send2, recv2, send3, recv3, *held,
):
    chunks, width, blocks, tile = raw.shape
    chips = groups // 2
    rows = stamp // groups
    planes = shards // chips
    steps = chunks * planes
    away = chunks * (planes - 1)
    cut_rows = width // planes
    k = lax.axis_index("chan")
    p = lax.axis_index("pix")
    x = k // 2
    y = lax.rem(p, chips)
    z = p // chips
    core = lax.rem(k, 2)
    other = 1 - core

    def fetch(t):
        n, j = t // planes, lax.rem(t, planes)
        lane = pl.multiple_of(n * tile, tile)
        here = pl.multiple_of(j * cut_rows, cut_rows)
        return pltpu.make_async_copy(
            sky_ref.at[pl.ds(here, cut_rows), :, pl.ds(lane, tile)], raw.at[n, pl.ds(here, cut_rows)], sky_sem.at[t]
        )

    sources = (owner_ref, ranks_ref, starts_ref, over_ref.at[p], gain_ref, coarse_ref, fine_ref)
    targets = (owner, ranks.at[0], starts.at[0], over, gain, coarse, fine)
    args = [pltpu.make_async_copy(a, b, arg_sem.at[i]) for i, (a, b) in enumerate(zip(sources, targets))]

    barrier = pltpu.get_barrier_semaphore()

    def greet(to_k, to_p):
        pl.semaphore_signal(barrier, inc=1, device_id=(to_k, to_p), device_id_type=MESH)

    for e in range(1, groups):
        greet(lax.rem(k + e, groups), p)
    for d in range(1, shards):
        greet(k, lax.rem(p + d, shards))
    for i in range(1, chips):
        for j in range(1, planes):
            greet(lax.rem(x + i, chips) * 2 + core, lax.rem(z + j, planes) * chips + y)
    peers = groups + shards - 2 + (chips - 1) * (planes - 1)
    for copy in args:
        copy.start()

    @pl.loop(0, steps)
    def _(t):
        fetch(t).start()

    def to_peer(e):
        pairs = ((ranks_ref, ranks), (starts_ref, starts))
        return [
            pltpu.make_async_remote_copy(
                src_ref=a,
                dst_ref=b.at[e],
                send_sem=send_l.at[e - 1, i],
                recv_sem=recv_l.at[e - 1, i],
                device_id=(lax.rem(k + e, groups), p),
                device_id_type=MESH,
            )
            for i, (a, b) in enumerate(pairs)
        ]

    def transpose(n, j):
        for i in range(cut_rows // 16):
            here = pl.multiple_of(j * cut_rows + 16 * i, 16)
            for b in range(0, blocks, 16):
                held[n][b : b + 16, pl.ds(here, 16), :] = jnp.swapaxes(raw[n, pl.ds(here, 16), b : b + 16, :], 0, 1)

    def to_core(t):
        return pltpu.make_async_remote_copy(
            src_ref=part.at[t],
            dst_ref=pair.at[t],
            send_sem=send0.at[t],
            recv_sem=recv0.at[t],
            device_id=(x * 2 + other, p),
            device_id_type=MESH,
        )

    def by_x(t):
        return lax.rem(t, 2) == 0

    def place(t):
        return jnp.where(by_x(t), x, y), jnp.where(by_x(t), y, x)

    def device(t, f, g, plane):
        to_x, to_y = jnp.where(by_x(t), f, g), jnp.where(by_x(t), g, f)
        return to_x * 2 + core, plane * chips + to_y

    def to_first(t, j):
        f, g = place(t)
        return pltpu.make_async_remote_copy(
            src_ref=mid1.at[t, j - 1],
            dst_ref=near1.at[t, j - 1],
            send_sem=send1.at[t, j - 1],
            recv_sem=recv1.at[t, j - 1],
            device_id=device(t, lax.rem(f + j, chips), g, z),
            device_id_type=MESH,
        )

    def to_second(t, j):
        f, g = place(t)
        return pltpu.make_async_remote_copy(
            src_ref=mid2.at[t, j - 1],
            dst_ref=near2.at[t, j - 1],
            send_sem=send2.at[t, j - 1],
            recv_sem=recv2.at[t, j - 1],
            device_id=device(t, f, lax.rem(g + j, chips), z),
            device_id_type=MESH,
        )

    def to_plane(t):
        f, g = place(t)
        plane = lax.rem(z + 1 + lax.rem(t, planes - 1), planes)
        return pltpu.make_async_remote_copy(
            src_ref=last.at[t],
            dst_ref=far.at[t],
            send_sem=send3.at[t],
            recv_sem=recv3.at[t],
            device_id=device(t, f, g, plane),
            device_id_type=MESH,
        )

    def compute(n, t, plane):
        for r in range(chips):
            q = plane * chips + r
            found = [held[n][jnp.maximum(lists_s[e, s, q], 0)] for e in range(groups) for s in range(slots)]
            total = jnp.dot(cuts[q], jnp.concatenate(found, axis=0), preferred_element_type=jnp.float32)
            total = total.reshape(chips, 2, rows, tile)
            mine = jnp.where(core == 0, total[:, 0], total[:, 1])
            sent = jnp.where(core == 0, total[:, 1], total[:, 0]).astype(jnp.bfloat16)
            for i in range(chips):
                f, g = jnp.where(by_x(t), i, r), jnp.where(by_x(t), r, i)
                kept[t, f, g] = mine[i]
                part[t, f, g] = sent[i]

    def first_stage(t):
        to_core(t).wait_recv()
        f, _ = place(t)
        for j in range(1, chips):
            to = lax.rem(f + j, chips)
            mid1[t, j - 1] = (kept[t, to] + pair[t, to].astype(jnp.float32)).astype(jnp.bfloat16)
            to_first(t, j).start()
        keep1[t] = kept[t, f] + pair[t, f].astype(jnp.float32)

    def first_sum(t, g):
        total = keep1[t, g]
        for j in range(1, chips):
            total += near1[t, j - 1, g].astype(jnp.float32)
        return total

    def second_stage(t):
        _, g = place(t)
        for j in range(1, chips):
            to_first(t, j).wait_recv()

        for j in range(1, chips):
            mid2[t, j - 1] = first_sum(t, lax.rem(g + j, chips)).astype(jnp.bfloat16)
            to_second(t, j).start()
        keep2[t] = first_sum(t, g)

    def third_stage(t):
        total = keep2[t]
        for j in range(1, chips):
            to_second(t, j).wait_recv()
            total += near2[t, j - 1].astype(jnp.float32)

        @pl.when(t < away)
        def _():
            last[t] = total.astype(jnp.bfloat16)
            to_plane(t).start()

        @pl.when(t >= away)
        def _():
            own[t - away] = total

    lists[...] = jnp.zeros_like(lists)
    over_v[...] = jnp.zeros_like(over_v)
    pl.semaphore_wait(barrier, peers)
    for e in range(1, groups):
        for copy in to_peer(e):
            copy.start()
    for copy in args:
        copy.wait()
    for c in range(groups):
        over_v[c * slots : (c + 1) * slots, :shards] = over[c]
    over_copy = pltpu.make_async_copy(over_v, over_s, local.at[0])
    over_copy.start()
    diff, add = filter_kernels(gain[...], coarse[...], fine[...])
    fill_filter(k * width, diff, add, filt)

    for n in range(PRE):
        @pl.loop(0, planes)
        def _(j, n=n):
            fetch(n * planes + j).wait()
            transpose(n, j)

    for e in range(1, groups):
        for copy in to_peer(e):
            copy.wait_recv()
    resolve(k, owner, ranks, starts, lists)
    lists_copy = pltpu.make_async_copy(lists, lists_s, local.at[1])
    lists_copy.start()
    over_copy.wait()
    lists_copy.wait()

    @pl.loop(0, shards)
    def _(q):
        for e in range(groups):
            c = lax.rem(k + groups - e, groups)
            for s in range(slots):
                first = lists_s[e, slots + s, q]
                weight = jnp.where(lists_s[e, s, q] >= 0, over_s[c * slots + s, q], 0.0)
                at = (e * slots + s) * width
                for h in range(width // LANES):
                    rows_h = weight * filt[h, pl.ds(first, stamp), :]
                    cuts[q, :, at + h * LANES : at + (h + 1) * LANES] = rows_h.astype(jnp.bfloat16)

    def stages(t):
        @pl.when((t >= LAG1) & (t < steps + LAG1))
        def _():
            first_stage(t - LAG1)

        @pl.when((t >= LAG2) & (t < steps + LAG2))
        def _():
            second_stage(t - LAG2)

        @pl.when(t >= LAG3)
        def _():
            third_stage(t - LAG3)

    def work(n, t, plane):
        compute(n, t, plane)
        to_core(t).start()
        stages(t)

    for n in range(chunks):
        @pl.loop(0, planes - 1)
        def _(j, n=n):
            if n + PRE < chunks:
                fetch((n + PRE) * planes + j).wait()
                transpose(n + PRE, j)

                @pl.when(j == planes - 2)
                def _():
                    fetch((n + PRE) * planes + j + 1).wait()
                    transpose(n + PRE, j + 1)

            work(n, n * (planes - 1) + j, lax.rem(z + 1 + j, planes))

    for n in range(chunks):
        work(n, away + n, z)

    @pl.loop(steps, steps + LAG3)
    def _(t):
        stages(t)

    for n in range(chunks):
        total = own[n]
        for j in range(planes - 1):
            t = n * (planes - 1) + j
            to_plane(t).wait_recv()
            total += far[t].astype(jnp.float32)
        out_ref[:, n * tile : (n + 1) * tile] = total

    for e in range(1, groups):
        for copy in to_peer(e):
            copy.wait_send()

    @pl.loop(0, steps)
    def _(t):
        to_core(t).wait_send()
        for j in range(1, chips):
            to_first(t, j).wait_send()
            to_second(t, j).wait_send()

        @pl.when(t < away)
        def _():
            to_plane(t).wait_send()


def body(sky_map, owner, stamp_block, chan_start, overdensity, delay_gain, *, groups, shards):
    width, blocks, pixels = sky_map.shape
    stamp = 128
    chips = groups // 2
    rows = stamp // groups
    slots = stamp_block.shape[3]
    size = delay_gain.shape[0]
    chunks = pixels // TILE
    planes = shards // chips
    steps = chunks * planes
    left, right = angle_tables(size)

    dma = pltpu.SemaphoreType.DMA
    f32, bf16, i32 = jnp.float32, jnp.bfloat16, jnp.int32
    vmem = pltpu.VMEM
    out = pl.pallas_call(
        functools.partial(stack_kernel, groups, shards, slots, stamp),
        out_shape=jax.ShapeDtypeStruct((rows, pixels), f32),
        in_specs=[pl.BlockSpec(memory_space=pl.ANY)] * 8,
        out_specs=pl.BlockSpec(memory_space=pltpu.VMEM),
        scratch_shapes=[
            vmem((1, blocks), i32),
            vmem((groups, slots, shards), i32),
            vmem((groups, slots, shards), i32),
            vmem((groups, slots, shards), f32),
            vmem((1, size), f32),
            vmem(left.shape, f32),
            vmem(right.shape, f32),
            dma((7,)),
            vmem((chunks, width, blocks, TILE), bf16),
            dma((steps,)),
            vmem((groups, 8, LANES), i32),
            pltpu.SMEM((groups, 8, LANES), i32),
            vmem((max(8, groups * slots), LANES), f32),
            pltpu.SMEM((max(8, groups * slots), LANES), f32),
            dma((2,)),
            dma((groups - 1, 2)),
            dma((groups - 1, 2)),
            vmem((width // LANES, size, LANES), f32),
            vmem((shards, stamp, groups * slots * width), bf16),
            vmem((steps, chips, chips, rows, TILE), bf16),
            vmem((steps, chips, chips, rows, TILE), f32),
            vmem((steps, chips, chips, rows, TILE), bf16),
            vmem((steps, chips - 1, chips, rows, TILE), bf16),
            vmem((steps, chips - 1, chips, rows, TILE), bf16),
            vmem((steps, chips, rows, TILE), f32),
            vmem((steps, chips - 1, rows, TILE), bf16),
            vmem((steps, chips - 1, rows, TILE), bf16),
            vmem((steps, rows, TILE), f32),
            vmem((chunks * (planes - 1), rows, TILE), bf16),
            vmem((chunks * (planes - 1), rows, TILE), bf16),
            vmem((chunks, rows, TILE), f32),
            dma((steps,)),
            dma((steps,)),
            dma((steps, chips - 1)),
            dma((steps, chips - 1)),
            dma((steps, chips - 1)),
            dma((steps, chips - 1)),
            dma((chunks * (planes - 1),)),
            dma((chunks * (planes - 1),)),
        ]
        + [vmem((blocks, width, TILE), bf16)] * chunks,
        compiler_params=pltpu.CompilerParams(
            collective_id=0, has_side_effects=True, vmem_limit_bytes=58 << 20
        ),
        name="stack_stamps",
    )(
        owner.reshape(1, blocks),
        stamp_block[0, 0].T,
        chan_start[0, 0].T,
        jnp.swapaxes(overdensity, 2, 3),
        delay_gain.reshape(1, size),
        left,
        right,
        sky_map,
    )
    return out[None]


def solution(mesh):
    in_specs = (
        P("chan", "pix", None),
        P("pix"),
        P("pix", "chan", None, None),
        P("pix", "chan", None, None),
        P(),
        P(),
    )
    run = functools.partial(body, groups=mesh.shape["chan"], shards=mesh.shape["pix"])
    return jax.shard_map(run, mesh=mesh, in_specs=in_specs, out_specs=P("pix", "chan", None), check_vma=False)
```

```python
import functools

import jax
import jax.numpy as jnp
import numpy as np
from jax import lax
from jax.experimental import pallas as pl
from jax.experimental.pallas import tpu as pltpu
from jax.sharding import PartitionSpec as P

MESH = pl.DeviceIdType.MESH
LANES = 128
TILE = 512
PRE = 1
LAG1 = 1
LAG2 = 5


def angle_tables(size):
    half = size // 2
    mode = np.arange(half)
    coarse = 2.0 * np.pi * ((mode[None, :] * np.arange(size // LANES)[:, None] * LANES) % size) / size
    fine = 2.0 * np.pi * ((mode[:, None] * np.arange(LANES)[None, :]) % size) / size
    left = np.concatenate([np.cos(coarse), -np.sin(coarse)], axis=1)
    right = np.concatenate([np.cos(fine), np.sin(fine)], axis=0) / size
    return left.astype(np.float32), right.astype(np.float32)


def filter_kernels(gain, coarse, fine):
    size = gain.shape[1]
    half = size // 2
    lanes = size // LANES
    even = gain[:, :half]
    odd = gain[:, half:]
    mode = lax.broadcasted_iota(jnp.int32, (1, half), 1)
    odd = jnp.where(mode == 0, 0.0, odd)
    plus = even + odd
    minus = jnp.where(mode == 0, 0.0, even - odd)
    plus = jnp.concatenate([plus, plus], axis=1)
    minus = jnp.concatenate([minus, minus], axis=1)
    left = jnp.concatenate([coarse * plus, coarse * minus], axis=0)
    out = jnp.dot(left, fine, precision=lax.Precision.HIGHEST, preferred_element_type=jnp.float32)
    sign = jnp.where(lax.rem(lax.broadcasted_iota(jnp.int32, (1, LANES), 1), 2) == 0, 1.0 / size, -1.0 / size)
    last = gain[:, half : half + 1] * sign
    diff = [jnp.broadcast_to(out[a : a + 1] + last, (8, LANES)) for a in range(lanes)]
    add = [jnp.broadcast_to(out[lanes + a : lanes + a + 1], (8, LANES)) for a in range(lanes)]
    return jnp.concatenate(diff, axis=1), jnp.concatenate(add, axis=1)


def fill_filter(first, diff, add, filt):
    size = diff.shape[1]
    halves = filt.shape[0]
    row = lax.broadcasted_iota(jnp.int32, (8, size), 0)
    back = lax.rem(size - first, size)
    diff = pltpu.roll(diff, back, 1)
    add = pltpu.roll(add, back, 1)
    diff_rows, add_rows = diff, add
    for i in range(1, 8):
        diff_rows = jnp.where(row == i, pltpu.roll(diff, i, 1), diff_rows)
        add_rows = jnp.where(row == i, pltpu.roll(add, size - i, 1), add_rows)
    lanes = size // LANES
    for v in range(LANES // 8):
        right = pltpu.roll(diff_rows, 8 * v, 1) if v else diff_rows
        left = pltpu.roll(add_rows, size - 8 * v, 1) if v else add_rows
        for u in range(lanes):
            for h in range(halves):
                a = (h - u) % lanes
                b = (h + u) % lanes
                rows = right[:, a * LANES : (a + 1) * LANES] + left[:, b * LANES : (b + 1) * LANES]
                rows = rows.astype(jnp.bfloat16).astype(jnp.float32)
                filt[h, u * LANES + 8 * v : u * LANES + 8 * v + 8, :] = rows


def resolve(k, owner, ranks, starts, lists):
    blocks = owner.shape[1]
    groups, slots, shards = ranks.shape
    row = lax.broadcasted_iota(jnp.int32, (blocks, blocks), 0)
    col = lax.broadcasted_iota(jnp.int32, (blocks, blocks), 1)
    across = jnp.broadcast_to(owner[...], (blocks, blocks))
    down = jnp.sum(jnp.where(row == col, across, 0), axis=1, keepdims=True)
    number = lax.broadcasted_iota(jnp.int32, (blocks, shards), 0) + 1
    rank = jnp.sum(jnp.where((across == down) & (col < row), 1, 0), axis=1, keepdims=True)
    for e in range(groups):
        c = lax.rem(k + groups - e, groups)
        held = jnp.broadcast_to(jnp.where(down == c, rank, -2), (blocks, shards))
        for s in range(slots):
            match = held == jnp.broadcast_to(ranks[e, s : s + 1], (blocks, shards))
            lists[e, s : s + 1, :shards] = jnp.sum(jnp.where(match, number, 0), axis=0, keepdims=True) - 1
        lists[e, slots : 2 * slots, :shards] = starts[e]


def stack_kernel(
    groups, shards, slots, stamp, owner_ref, ranks_ref, starts_ref, over_ref, gain_ref, coarse_ref, fine_ref, sky_ref, out_ref,
    owner, ranks, starts, over, gain, coarse, fine, arg_sem, raw, sky_sem, lists, lists_s, over_v, over_s, local, send_l, recv_l,
    filt, cuts, part, kept, pair, mid, near, keep, last, far, own,
    send0, recv0, send1, recv1, send2, recv2, *held,
):
    chunks, width, blocks, tile = raw.shape
    chips = groups // 2
    rows = stamp // groups
    planes = shards // chips
    steps = chunks * planes
    away = chunks * (planes - 1)
    cut_rows = width // planes
    k = lax.axis_index("chan")
    p = lax.axis_index("pix")
    x = k // 2
    y = lax.rem(p, chips)
    z = p // chips
    core = lax.rem(k, 2)
    other = 1 - core

    def fetch(t):
        n, j = t // planes, lax.rem(t, planes)
        lane = pl.multiple_of(n * tile, tile)
        here = pl.multiple_of(j * cut_rows, cut_rows)
        return pltpu.make_async_copy(
            sky_ref.at[pl.ds(here, cut_rows), :, pl.ds(lane, tile)], raw.at[n, pl.ds(here, cut_rows)], sky_sem.at[t]
        )

    sources = (owner_ref, ranks_ref, starts_ref, over_ref.at[p], gain_ref, coarse_ref, fine_ref)
    targets = (owner, ranks.at[0], starts.at[0], over, gain, coarse, fine)
    args = [pltpu.make_async_copy(a, b, arg_sem.at[i]) for i, (a, b) in enumerate(zip(sources, targets))]

    barrier = pltpu.get_barrier_semaphore()

    def greet(to_k, to_p):
        pl.semaphore_signal(barrier, inc=1, device_id=(to_k, to_p), device_id_type=MESH)

    for e in range(1, groups):
        greet(lax.rem(k + e, groups), p)
    for d in range(1, shards):
        greet(k, lax.rem(p + d, shards))
    for i in range(1, chips):
        for j in range(1, chips):
            greet(lax.rem(x + i, chips) * 2 + core, z * chips + lax.rem(y + j, chips))
    peers = groups + shards - 2 + (chips - 1) * (chips - 1)
    for copy in args:
        copy.start()

    @pl.loop(0, steps)
    def _(t):
        fetch(t).start()

    def to_peer(e):
        pairs = ((ranks_ref, ranks), (starts_ref, starts))
        return [
            pltpu.make_async_remote_copy(
                src_ref=a,
                dst_ref=b.at[e],
                send_sem=send_l.at[e - 1, i],
                recv_sem=recv_l.at[e - 1, i],
                device_id=(lax.rem(k + e, groups), p),
                device_id_type=MESH,
            )
            for i, (a, b) in enumerate(pairs)
        ]

    def transpose(n, j):
        for i in range(cut_rows // 16):
            here = pl.multiple_of(j * cut_rows + 16 * i, 16)
            for b in range(0, blocks, 16):
                held[n][b : b + 16, pl.ds(here, 16), :] = jnp.swapaxes(raw[n, pl.ds(here, 16), b : b + 16, :], 0, 1)

    def to_core(t):
        return pltpu.make_async_remote_copy(
            src_ref=part.at[t],
            dst_ref=pair.at[t],
            send_sem=send0.at[t],
            recv_sem=recv0.at[t],
            device_id=(x * 2 + other, p),
            device_id_type=MESH,
        )

    def mate(i):
        return lax.rem(x + i // chips, chips), lax.rem(y + i % chips, chips)

    def to_mate(t, i):
        to_x, to_y = mate(i)
        return pltpu.make_async_remote_copy(
            src_ref=mid.at[t, i - 1],
            dst_ref=near.at[t, i - 1],
            send_sem=send1.at[t, i - 1],
            recv_sem=recv1.at[t, i - 1],
            device_id=(to_x * 2 + core, z * chips + to_y),
            device_id_type=MESH,
        )

    def to_plane(t):
        plane = lax.rem(z + 1 + lax.rem(t, planes - 1), planes)
        return pltpu.make_async_remote_copy(
            src_ref=last.at[t],
            dst_ref=far.at[t],
            send_sem=send2.at[t],
            recv_sem=recv2.at[t],
            device_id=(k, plane * chips + y),
            device_id_type=MESH,
        )

    def compute(n, t, plane):
        for r in range(chips):
            q = plane * chips + r
            found = [held[n][jnp.maximum(lists_s[e, s, q], 0)] for e in range(groups) for s in range(slots)]
            total = jnp.dot(cuts[q], jnp.concatenate(found, axis=0), preferred_element_type=jnp.float32)
            total = total.reshape(chips, 2, rows, tile)
            mine = jnp.where(core == 0, total[:, 0], total[:, 1])
            sent = jnp.where(core == 0, total[:, 1], total[:, 0]).astype(jnp.bfloat16)
            kept[t, r] = mine
            part[t, r] = sent

    def first_stage(t):
        to_core(t).wait_recv()
        for i in range(1, chips * chips):
            to_x, to_y = mate(i)
            mid[t, i - 1] = (kept[t, to_y, to_x] + pair[t, to_y, to_x].astype(jnp.float32)).astype(jnp.bfloat16)
            to_mate(t, i).start()
        keep[t] = kept[t, y, x] + pair[t, y, x].astype(jnp.float32)

    def second_stage(t):
        total = keep[t]
        for i in range(1, chips * chips):
            to_mate(t, i).wait_recv()
            total += near[t, i - 1].astype(jnp.float32)

        @pl.when(t < away)
        def _():
            last[t] = total.astype(jnp.bfloat16)
            to_plane(t).start()

        @pl.when(t >= away)
        def _():
            own[t - away] = total

    lists[...] = jnp.zeros_like(lists)
    over_v[...] = jnp.zeros_like(over_v)
    for copy in args:
        copy.wait()
    for c in range(groups):
        over_v[c * slots : (c + 1) * slots, :shards] = over[c]
    over_copy = pltpu.make_async_copy(over_v, over_s, local.at[0])
    over_copy.start()
    diff, add = filter_kernels(gain[...], coarse[...], fine[...])
    fill_filter(k * width, diff, add, filt)
    pl.semaphore_wait(barrier, peers)
    for e in range(1, groups):
        for copy in to_peer(e):
            copy.start()

    for n in range(PRE):
        @pl.loop(0, planes)
        def _(j, n=n):
            fetch(n * planes + j).wait()
            transpose(n, j)

    for e in range(1, groups):
        for copy in to_peer(e):
            copy.wait_recv()
    resolve(k, owner, ranks, starts, lists)
    lists_copy = pltpu.make_async_copy(lists, lists_s, local.at[1])
    lists_copy.start()
    over_copy.wait()
    lists_copy.wait()

    @pl.loop(0, shards)
    def _(q):
        for e in range(groups):
            c = lax.rem(k + groups - e, groups)
            for s in range(slots):
                first = lists_s[e, slots + s, q]
                weight = jnp.where(lists_s[e, s, q] >= 0, over_s[c * slots + s, q], 0.0)
                at = (e * slots + s) * width
                for h in range(width // LANES):
                    rows_h = weight * filt[h, pl.ds(first, stamp), :]
                    cuts[q, :, at + h * LANES : at + (h + 1) * LANES] = rows_h.astype(jnp.bfloat16)

    def stages(t):
        @pl.when((t >= LAG1) & (t < steps + LAG1))
        def _():
            first_stage(t - LAG1)

        @pl.when(t >= LAG2)
        def _():
            second_stage(t - LAG2)

    def work(n, t, plane):
        compute(n, t, plane)
        to_core(t).start()
        stages(t)

    for n in range(chunks):
        @pl.loop(0, planes - 1)
        def _(j, n=n):
            if n + PRE < chunks:
                fetch((n + PRE) * planes + j).wait()
                transpose(n + PRE, j)

                @pl.when(j == planes - 2)
                def _():
                    fetch((n + PRE) * planes + j + 1).wait()
                    transpose(n + PRE, j + 1)

            work(n, n * (planes - 1) + j, lax.rem(z + 1 + j, planes))

    for n in range(chunks):
        work(n, away + n, z)

    @pl.loop(steps, steps + LAG2)
    def _(t):
        stages(t)

    for n in range(chunks):
        total = own[n]
        for j in range(planes - 1):
            t = n * (planes - 1) + j
            to_plane(t).wait_recv()
            total += far[t].astype(jnp.float32)
        out_ref[:, n * tile : (n + 1) * tile] = total

    for e in range(1, groups):
        for copy in to_peer(e):
            copy.wait_send()

    @pl.loop(0, steps)
    def _(t):
        to_core(t).wait_send()
        for i in range(1, chips * chips):
            to_mate(t, i).wait_send()

        @pl.when(t < away)
        def _():
            to_plane(t).wait_send()


def body(sky_map, owner, stamp_block, chan_start, overdensity, delay_gain, *, groups, shards):
    width, blocks, pixels = sky_map.shape
    stamp = 128
    chips = groups // 2
    rows = stamp // groups
    slots = stamp_block.shape[3]
    size = delay_gain.shape[0]
    chunks = pixels // TILE
    planes = shards // chips
    steps = chunks * planes
    left, right = angle_tables(size)

    dma = pltpu.SemaphoreType.DMA
    f32, bf16, i32 = jnp.float32, jnp.bfloat16, jnp.int32
    vmem = pltpu.VMEM
    out = pl.pallas_call(
        functools.partial(stack_kernel, groups, shards, slots, stamp),
        out_shape=jax.ShapeDtypeStruct((rows, pixels), f32),
        in_specs=[pl.BlockSpec(memory_space=pl.ANY)] * 8,
        out_specs=pl.BlockSpec(memory_space=pltpu.VMEM),
        scratch_shapes=[
            vmem((1, blocks), i32),
            vmem((groups, slots, shards), i32),
            vmem((groups, slots, shards), i32),
            vmem((groups, slots, shards), f32),
            vmem((1, size), f32),
            vmem(left.shape, f32),
            vmem(right.shape, f32),
            dma((7,)),
            vmem((chunks, width, blocks, TILE), bf16),
            dma((steps,)),
            vmem((groups, 8, LANES), i32),
            pltpu.SMEM((groups, 8, LANES), i32),
            vmem((max(8, groups * slots), LANES), f32),
            pltpu.SMEM((max(8, groups * slots), LANES), f32),
            dma((2,)),
            dma((groups - 1, 2)),
            dma((groups - 1, 2)),
            vmem((width // LANES, size, LANES), f32),
            vmem((shards, stamp, groups * slots * width), bf16),
            vmem((steps, chips, chips, rows, TILE), bf16),
            vmem((steps, chips, chips, rows, TILE), f32),
            vmem((steps, chips, chips, rows, TILE), bf16),
            vmem((steps, chips * chips - 1, rows, TILE), bf16),
            vmem((steps, chips * chips - 1, rows, TILE), bf16),
            vmem((steps, rows, TILE), f32),
            vmem((chunks * (planes - 1), rows, TILE), bf16),
            vmem((chunks * (planes - 1), rows, TILE), bf16),
            vmem((chunks, rows, TILE), f32),
            dma((steps,)),
            dma((steps,)),
            dma((steps, chips * chips - 1)),
            dma((steps, chips * chips - 1)),
            dma((chunks * (planes - 1),)),
            dma((chunks * (planes - 1),)),
        ]
        + [vmem((blocks, width, TILE), bf16)] * chunks,
        compiler_params=pltpu.CompilerParams(
            collective_id=0, has_side_effects=True, vmem_limit_bytes=58 << 20
        ),
        name="stack_stamps",
    )(
        owner.reshape(1, blocks),
        stamp_block[0, 0].T,
        chan_start[0, 0].T,
        jnp.swapaxes(overdensity, 2, 3),
        delay_gain.reshape(1, size),
        left,
        right,
        sky_map,
    )
    return out[None]


def solution(mesh):
    in_specs = (
        P("chan", "pix", None),
        P("pix"),
        P("pix", "chan", None, None),
        P("pix", "chan", None, None),
        P(),
        P(),
    )
    run = functools.partial(body, groups=mesh.shape["chan"], shards=mesh.shape["pix"])
    return jax.shard_map(run, mesh=mesh, in_specs=in_specs, out_specs=P("pix", "chan", None), check_vma=False)
```

```python
import functools

import jax
import jax.numpy as jnp
import numpy as np
from jax import lax
from jax.experimental import pallas as pl
from jax.experimental.pallas import tpu as pltpu
from jax.sharding import PartitionSpec as P

MESH = pl.DeviceIdType.MESH
LANES = 128
TILE = 512
PRE = 1
LAG1 = 1
LAG2 = 5


def angle_tables(size):
    half = size // 2
    mode = np.arange(half)
    coarse = 2.0 * np.pi * ((mode[None, :] * np.arange(size // LANES)[:, None] * LANES) % size) / size
    fine = 2.0 * np.pi * ((mode[:, None] * np.arange(LANES)[None, :]) % size) / size
    left = np.concatenate([np.cos(coarse), -np.sin(coarse)], axis=1)
    right = np.concatenate([np.cos(fine), np.sin(fine)], axis=0) / size
    return left.astype(np.float32), right.astype(np.float32)


def filter_kernels(gain, coarse, fine):
    size = gain.shape[1]
    half = size // 2
    lanes = size // LANES
    even = gain[:, :half]
    odd = gain[:, half:]
    mode = lax.broadcasted_iota(jnp.int32, (1, half), 1)
    odd = jnp.where(mode == 0, 0.0, odd)
    plus = even + odd
    minus = jnp.where(mode == 0, 0.0, even - odd)
    plus = jnp.concatenate([plus, plus], axis=1)
    minus = jnp.concatenate([minus, minus], axis=1)
    left = jnp.concatenate([coarse * plus, coarse * minus], axis=0)
    out = jnp.dot(left, fine, precision=lax.Precision.HIGHEST, preferred_element_type=jnp.float32)
    sign = jnp.where(lax.rem(lax.broadcasted_iota(jnp.int32, (1, LANES), 1), 2) == 0, 1.0 / size, -1.0 / size)
    last = gain[:, half : half + 1] * sign
    diff = [jnp.broadcast_to(out[a : a + 1] + last, (8, LANES)) for a in range(lanes)]
    add = [jnp.broadcast_to(out[lanes + a : lanes + a + 1], (8, LANES)) for a in range(lanes)]
    return jnp.concatenate(diff, axis=1), jnp.concatenate(add, axis=1)


def fill_filter(first, diff, add, filt):
    size = diff.shape[1]
    halves = filt.shape[0]
    row = lax.broadcasted_iota(jnp.int32, (8, size), 0)
    back = lax.rem(size - first, size)
    diff = pltpu.roll(diff, back, 1)
    add = pltpu.roll(add, back, 1)
    diff_rows, add_rows = diff, add
    for i in range(1, 8):
        diff_rows = jnp.where(row == i, pltpu.roll(diff, i, 1), diff_rows)
        add_rows = jnp.where(row == i, pltpu.roll(add, size - i, 1), add_rows)
    lanes = size // LANES
    for v in range(LANES // 8):
        right = pltpu.roll(diff_rows, 8 * v, 1) if v else diff_rows
        left = pltpu.roll(add_rows, size - 8 * v, 1) if v else add_rows
        for u in range(lanes):
            for h in range(halves):
                a = (h - u) % lanes
                b = (h + u) % lanes
                rows = right[:, a * LANES : (a + 1) * LANES] + left[:, b * LANES : (b + 1) * LANES]
                rows = rows.astype(jnp.bfloat16).astype(jnp.float32)
                filt[h, u * LANES + 8 * v : u * LANES + 8 * v + 8, :] = rows


def resolve(k, owner, ranks, starts, lists):
    blocks = owner.shape[1]
    groups, slots, shards = ranks.shape
    row = lax.broadcasted_iota(jnp.int32, (blocks, blocks), 0)
    col = lax.broadcasted_iota(jnp.int32, (blocks, blocks), 1)
    across = jnp.broadcast_to(owner[...], (blocks, blocks))
    down = jnp.sum(jnp.where(row == col, across, 0), axis=1, keepdims=True)
    number = lax.broadcasted_iota(jnp.int32, (blocks, shards), 0) + 1
    rank = jnp.sum(jnp.where((across == down) & (col < row), 1, 0), axis=1, keepdims=True)
    for e in range(groups):
        c = lax.rem(k + groups - e, groups)
        held = jnp.broadcast_to(jnp.where(down == c, rank, -2), (blocks, shards))
        for s in range(slots):
            match = held == jnp.broadcast_to(ranks[e, s : s + 1], (blocks, shards))
            lists[e, s : s + 1, :shards] = jnp.sum(jnp.where(match, number, 0), axis=0, keepdims=True) - 1
        lists[e, slots : 2 * slots, :shards] = starts[e]


def stack_kernel(
    groups, shards, slots, stamp, owner_ref, ranks_ref, starts_ref, over_ref, gain_ref, coarse_ref, fine_ref, sky_ref, out_ref,
    owner, ranks, starts, over, gain, coarse, fine, arg_sem, raw, sky_sem, lists, lists_s, over_v, over_s, local, send_l, recv_l,
    filt, cuts, part, kept, pair, mid, near, keep, last, far, own,
    send0, recv0, send1, recv1, send2, recv2, *held,
):
    chunks, width, blocks, tile = raw.shape
    chips = groups // 2
    rows = stamp // groups
    planes = shards // chips
    steps = chunks * planes
    away = chunks * (planes - 1)
    cut_rows = width // planes
    k = lax.axis_index("chan")
    p = lax.axis_index("pix")
    x = k // 2
    y = lax.rem(p, chips)
    z = p // chips
    core = lax.rem(k, 2)
    other = 1 - core

    def fetch(t):
        n, j = t // planes, lax.rem(t, planes)
        lane = pl.multiple_of(n * tile, tile)
        here = pl.multiple_of(j * cut_rows, cut_rows)
        return pltpu.make_async_copy(
            sky_ref.at[pl.ds(here, cut_rows), :, pl.ds(lane, tile)], raw.at[n, pl.ds(here, cut_rows)], sky_sem.at[t]
        )

    sources = (owner_ref, ranks_ref, starts_ref, over_ref.at[p], gain_ref, coarse_ref, fine_ref)
    targets = (owner, ranks.at[0], starts.at[0], over, gain, coarse, fine)
    args = [pltpu.make_async_copy(a, b, arg_sem.at[i]) for i, (a, b) in enumerate(zip(sources, targets))]

    barrier = pltpu.get_barrier_semaphore()

    def greet(to_k, to_p):
        pl.semaphore_signal(barrier, inc=1, device_id=(to_k, to_p), device_id_type=MESH)

    for e in range(1, groups):
        greet(lax.rem(k + e, groups), p)
    for d in range(1, shards):
        greet(k, lax.rem(p + d, shards))
    for i in range(1, chips):
        for j in range(1, chips):
            greet(lax.rem(x + i, chips) * 2 + core, z * chips + lax.rem(y + j, chips))
    peers = groups + shards - 2 + (chips - 1) * (chips - 1)
    for copy in args:
        copy.start()

    @pl.loop(0, steps)
    def _(t):
        fetch(t).start()

    def to_peer(e):
        pairs = ((ranks_ref, ranks), (starts_ref, starts))
        return [
            pltpu.make_async_remote_copy(
                src_ref=a,
                dst_ref=b.at[e],
                send_sem=send_l.at[e - 1, i],
                recv_sem=recv_l.at[e - 1, i],
                device_id=(lax.rem(k + e, groups), p),
                device_id_type=MESH,
            )
            for i, (a, b) in enumerate(pairs)
        ]

    def transpose(n, j):
        for i in range(cut_rows // 16):
            here = pl.multiple_of(j * cut_rows + 16 * i, 16)
            for b in range(0, blocks, 16):
                held[n][b : b + 16, pl.ds(here, 16), :] = jnp.swapaxes(raw[n, pl.ds(here, 16), b : b + 16, :], 0, 1)

    def to_core(t):
        return pltpu.make_async_remote_copy(
            src_ref=part.at[t],
            dst_ref=pair.at[t],
            send_sem=send0.at[t],
            recv_sem=recv0.at[t],
            device_id=(x * 2 + other, p),
            device_id_type=MESH,
        )

    def mate(i):
        return lax.rem(x + i // chips, chips), lax.rem(y + i % chips, chips)

    def to_mate(t, i):
        to_x, to_y = mate(i)
        return pltpu.make_async_remote_copy(
            src_ref=mid.at[t, i - 1],
            dst_ref=near.at[t, i - 1],
            send_sem=send1.at[t, i - 1],
            recv_sem=recv1.at[t, i - 1],
            device_id=(to_x * 2 + core, z * chips + to_y),
            device_id_type=MESH,
        )

    def to_plane(t):
        plane = lax.rem(z + 1 + lax.rem(t, planes - 1), planes)
        return pltpu.make_async_remote_copy(
            src_ref=last.at[t],
            dst_ref=far.at[t],
            send_sem=send2.at[t],
            recv_sem=recv2.at[t],
            device_id=(k, plane * chips + y),
            device_id_type=MESH,
        )

    def compute(n, t, plane):
        for r in range(chips):
            q = plane * chips + r
            found = [held[n][jnp.maximum(lists_s[e, s, q], 0)] for e in range(groups) for s in range(slots)]
            total = jnp.dot(cuts[q], jnp.concatenate(found, axis=0), preferred_element_type=jnp.float32)
            total = total.reshape(chips, 2, rows, tile)
            mine = jnp.where(core == 0, total[:, 0], total[:, 1])
            sent = jnp.where(core == 0, total[:, 1], total[:, 0]).astype(jnp.bfloat16)
            kept[t, r] = mine
            part[t, r] = sent

    def first_stage(t):
        to_core(t).wait_recv()
        for i in range(1, chips * chips):
            to_x, to_y = mate(i)
            mid[t, i - 1] = (kept[t, to_y, to_x] + pair[t, to_y, to_x].astype(jnp.float32)).astype(jnp.bfloat16)
            to_mate(t, i).start()
        keep[t] = kept[t, y, x] + pair[t, y, x].astype(jnp.float32)

    def second_stage(t):
        total = keep[t]
        for i in range(1, chips * chips):
            to_mate(t, i).wait_recv()
            total += near[t, i - 1].astype(jnp.float32)

        @pl.when(t < away)
        def _():
            last[t] = total.astype(jnp.bfloat16)
            to_plane(t).start()

        @pl.when(t >= away)
        def _():
            own[t - away] = total

    lists[...] = jnp.zeros_like(lists)
    over_v[...] = jnp.zeros_like(over_v)
    for copy in args:
        copy.wait()
    for c in range(groups):
        over_v[c * slots : (c + 1) * slots, :shards] = over[c]
    over_copy = pltpu.make_async_copy(over_v, over_s, local.at[0])
    over_copy.start()
    diff, add = filter_kernels(gain[...], coarse[...], fine[...])
    fill_filter(k * width, diff, add, filt)
    pl.semaphore_wait(barrier, peers)
    for e in range(1, groups):
        for copy in to_peer(e):
            copy.start()

    for n in range(PRE):
        @pl.loop(0, planes)
        def _(j, n=n):
            fetch(n * planes + j).wait()
            transpose(n, j)

    for e in range(1, groups):
        for copy in to_peer(e):
            copy.wait_recv()
    resolve(k, owner, ranks, starts, lists)
    lists_copy = pltpu.make_async_copy(lists, lists_s, local.at[1])
    lists_copy.start()
    if PRE < chunks:
        fetch(PRE * planes).wait()
        transpose(PRE, 0)
    over_copy.wait()
    lists_copy.wait()

    @pl.loop(0, shards)
    def _(q):
        for e in range(groups):
            c = lax.rem(k + groups - e, groups)
            for s in range(slots):
                first = lists_s[e, slots + s, q]
                weight = jnp.where(lists_s[e, s, q] >= 0, over_s[c * slots + s, q], 0.0)
                at = (e * slots + s) * width
                for h in range(width // LANES):
                    rows_h = weight * filt[h, pl.ds(first, stamp), :]
                    cuts[q, :, at + h * LANES : at + (h + 1) * LANES] = rows_h.astype(jnp.bfloat16)

    def stages(t):
        @pl.when((t >= LAG1) & (t < steps + LAG1))
        def _():
            first_stage(t - LAG1)

        @pl.when(t >= LAG2)
        def _():
            second_stage(t - LAG2)

    def work(n, t, plane):
        compute(n, t, plane)
        to_core(t).start()
        stages(t)

    for n in range(chunks):
        if n and n + PRE < chunks:
            fetch((n + PRE) * planes).wait()
            transpose(n + PRE, 0)

        @pl.loop(0, planes - 1)
        def _(j, n=n):
            if n + PRE < chunks:
                fetch((n + PRE) * planes + j + 1).wait()
                transpose(n + PRE, j + 1)

            work(n, n * (planes - 1) + j, lax.rem(z + 1 + j, planes))

    for n in range(chunks):
        work(n, away + n, z)

    @pl.loop(steps, steps + LAG2)
    def _(t):
        stages(t)

    for n in range(chunks):
        total = own[n]
        for j in range(planes - 1):
            t = n * (planes - 1) + j
            to_plane(t).wait_recv()
            total += far[t].astype(jnp.float32)
        out_ref[:, n * tile : (n + 1) * tile] = total

    for e in range(1, groups):
        for copy in to_peer(e):
            copy.wait_send()

    @pl.loop(0, steps)
    def _(t):
        to_core(t).wait_send()
        for i in range(1, chips * chips):
            to_mate(t, i).wait_send()

        @pl.when(t < away)
        def _():
            to_plane(t).wait_send()


def body(sky_map, owner, stamp_block, chan_start, overdensity, delay_gain, *, groups, shards):
    width, blocks, pixels = sky_map.shape
    stamp = 128
    chips = groups // 2
    rows = stamp // groups
    slots = stamp_block.shape[3]
    size = delay_gain.shape[0]
    chunks = pixels // TILE
    planes = shards // chips
    steps = chunks * planes
    left, right = angle_tables(size)

    dma = pltpu.SemaphoreType.DMA
    f32, bf16, i32 = jnp.float32, jnp.bfloat16, jnp.int32
    vmem = pltpu.VMEM
    out = pl.pallas_call(
        functools.partial(stack_kernel, groups, shards, slots, stamp),
        out_shape=jax.ShapeDtypeStruct((rows, pixels), f32),
        in_specs=[pl.BlockSpec(memory_space=pl.ANY)] * 8,
        out_specs=pl.BlockSpec(memory_space=pltpu.VMEM),
        scratch_shapes=[
            vmem((1, blocks), i32),
            vmem((groups, slots, shards), i32),
            vmem((groups, slots, shards), i32),
            vmem((groups, slots, shards), f32),
            vmem((1, size), f32),
            vmem(left.shape, f32),
            vmem(right.shape, f32),
            dma((7,)),
            vmem((chunks, width, blocks, TILE), bf16),
            dma((steps,)),
            vmem((groups, 8, LANES), i32),
            pltpu.SMEM((groups, 8, LANES), i32),
            vmem((max(8, groups * slots), LANES), f32),
            pltpu.SMEM((max(8, groups * slots), LANES), f32),
            dma((2,)),
            dma((groups - 1, 2)),
            dma((groups - 1, 2)),
            vmem((width // LANES, size, LANES), f32),
            vmem((shards, stamp, groups * slots * width), bf16),
            vmem((steps, chips, chips, rows, TILE), bf16),
            vmem((steps, chips, chips, rows, TILE), f32),
            vmem((steps, chips, chips, rows, TILE), bf16),
            vmem((steps, chips * chips - 1, rows, TILE), bf16),
            vmem((steps, chips * chips - 1, rows, TILE), bf16),
            vmem((steps, rows, TILE), f32),
            vmem((chunks * (planes - 1), rows, TILE), bf16),
            vmem((chunks * (planes - 1), rows, TILE), bf16),
            vmem((chunks, rows, TILE), f32),
            dma((steps,)),
            dma((steps,)),
            dma((steps, chips * chips - 1)),
            dma((steps, chips * chips - 1)),
            dma((chunks * (planes - 1),)),
            dma((chunks * (planes - 1),)),
        ]
        + [vmem((blocks, width, TILE), bf16)] * chunks,
        compiler_params=pltpu.CompilerParams(
            collective_id=0, has_side_effects=True, vmem_limit_bytes=58 << 20
        ),
        name="stack_stamps",
    )(
        owner.reshape(1, blocks),
        stamp_block[0, 0].T,
        chan_start[0, 0].T,
        jnp.swapaxes(overdensity, 2, 3),
        delay_gain.reshape(1, size),
        left,
        right,
        sky_map,
    )
    return out[None]


def solution(mesh):
    in_specs = (
        P("chan", "pix", None),
        P("pix"),
        P("pix", "chan", None, None),
        P("pix", "chan", None, None),
        P(),
        P(),
    )
    run = functools.partial(body, groups=mesh.shape["chan"], shards=mesh.shape["pix"])
    return jax.shard_map(run, mesh=mesh, in_specs=in_specs, out_specs=P("pix", "chan", None), check_vma=False)
```
